32 devices in a mesh: layer: 4 (over z), tok: 8 (over y, x, core).
Axes of the slice: x: 2, y: 2, z: 4, core: 2. Of those that a mesh axis runs over, the one named last changes fastest.
Arguments:
- acts: bfloat16 [4, 8192, 4096], P('layer', 'tok'), may hold values from -48 to 48
- probe_weight: bfloat16 [4, 4096, 512], P('layer'), may hold values from -0.09375 to 0.09375
- mix_table: int32 [16, 2], replicated, may hold values from 0 to 3
- mix_scale: float32 [16], replicated, may hold values from 0.1 to 0.4
- labels: int32 [8192], P('tok'), may hold values from 0 to 511
Outputs:
- probe_grad: float32 [4, 4096, 512], P('layer', 'tok')
The draws below stay inside these ranges and needn't reach their ends.
All inputs are finite; a program needn't handle non-finite values.
Results may differ from the reference program's by a relative error of at most 0.0028.
Values may be sent and summed in bfloat16 or wider, within the bound.
A program may use at most 256 MiB of HBM per device.

```python
import math
import jax
import jax.numpy as jnp
from jax import lax

D = 4096
CLASSES = 512
PAIRS = 16
LAYERS = 4
TOKENS = 8192


def draw_acts(key, part):
    first = jax.random.fold_in(jax.random.fold_in(key, 11), 0)
    values = jax.random.truncated_normal(first, -6.0, 6.0, (LAYERS, TOKENS, D), jnp.float32)
    return values.astype(jnp.bfloat16)


def set_ends(drawn, stream_key, smallest, high):
    longest = drawn.shape.index(max(drawn.shape))
    spots = []
    for shift in (0, 1):
        where = [jax.random.randint(jax.random.fold_in(stream_key, axis), (), 0, length) for axis, length in enumerate(drawn.shape)]
        where[longest] = (where[longest] + shift) % drawn.shape[longest]
        spots.append(tuple(where))
    return drawn.at[spots[0]].set(smallest).at[spots[1]].set(high)


def block_levels(rng, shape, cuts, least, top_value):
    def one(axis_at, blocks):
        heights = jax.random.uniform(jax.random.fold_in(jax.random.fold_in(rng, 6), axis_at), (blocks,), jnp.float32, least / len(cuts), top_value / len(cuts))
        return jnp.repeat(jnp.exp(heights), shape[axis_at] // blocks).reshape((-1,) + (1,) * (len(shape) - axis_at - 1))

    level = one(*cuts[0])
    for cut in cuts[1:]:
        level = level * one(*cut)
    return level


def centred(rng, dims, width, reach, cuts=(), kind=jnp.bfloat16):
    factor_of = block_levels(rng, dims, cuts, -0.22, 0.18) if cuts else 1.0
    entries = jax.random.normal(rng, dims, jnp.float32) * width * factor_of
    return jnp.minimum(jnp.maximum(entries, -reach), reach).astype(kind)


def setup_inputs(seed: int = 0) -> dict:
    arg_keys = jax.random.split(jax.random.key(seed), 6)
    acts = draw_acts(jax.random.fold_in(arg_keys[5], 71), 0)
    probe_weight = centred(arg_keys[1], (LAYERS, D, CLASSES), D ** -0.5, 0.09375, ((0, 4),))
    mix_table = set_ends(jax.random.randint(arg_keys[2], (PAIRS, 2), 0, LAYERS), jax.random.fold_in(arg_keys[2], 1), 0, LAYERS - 1).astype(jnp.int32)
    mix_scale = jnp.clip(jnp.exp(jax.random.uniform(arg_keys[3], (PAIRS,), jnp.float32, math.log(0.1), math.log(0.4))), 0.1, 0.4)
    labels = set_ends(jax.random.randint(arg_keys[4], (TOKENS,), 0, CLASSES), jax.random.fold_in(arg_keys[4], 1), 0, CLASSES - 1).astype(jnp.int32)
    return dict(acts=acts, probe_weight=probe_weight, mix_table=mix_table, mix_scale=mix_scale, labels=labels)


def loss_grad(partial_value, labels, pick_a, pick_b, mix_scale, norm):
    classes = partial_value.shape[2]
    wide = partial_value.astype(jnp.float32)
    best = lax.Precision.HIGHEST
    first = jnp.einsum('ql,lnc->qnc', pick_a, wide, precision=best)
    second = jnp.einsum('ql,lnc->qnc', pick_b, wide, precision=best)
    logits = lax.optimization_barrier(jnp.sum(wide, axis=0)) + jnp.einsum('q,qnc->nc', mix_scale, first * second, precision=best)
    top = lax.optimization_barrier(jnp.max(logits, axis=1, keepdims=True))
    expo = jnp.exp(logits - top)
    probs = expo / lax.optimization_barrier(jnp.sum(expo, axis=1, keepdims=True))
    onehot = (labels[:, None] == jnp.arange(classes, dtype=jnp.int32)[None, :]).astype(jnp.float32)
    grad = (probs - onehot) * norm
    weighted_a = pick_a * mix_scale[:, None]
    weighted_b = pick_b * mix_scale[:, None]
    factor = jnp.einsum('ql,qnc->lnc', weighted_a, second, precision=best) + jnp.einsum('ql,qnc->lnc', weighted_b, first, precision=best)
    return (grad[None] * (1.0 + factor)).astype(jnp.bfloat16)

def reference(acts, probe_weight, mix_table, mix_scale, labels):
    layers = acts.shape[0]
    span = jnp.arange(layers, dtype=jnp.int32)[None, :]
    pick_a = (mix_table[:, 0:1] == span).astype(jnp.float32)
    pick_b = (mix_table[:, 1:2] == span).astype(jnp.float32)
    scale = mix_scale.astype(jnp.float32)

    def project(pair):
        return jnp.dot(pair[0], pair[1], preferred_element_type=jnp.float32)
    partial_value = lax.map(project, (acts, probe_weight))
    block = math.gcd(TOKENS, 512)
    count = TOKENS // block
    blocks = partial_value.reshape(layers, count, block, CLASSES).transpose(1, 0, 2, 3)
    label_blocks = labels.reshape(count, block)
    norm = 1.0 / math.sqrt(TOKENS)

    def one_block(pair):
        return loss_grad(pair[0], pair[1], pick_a, pick_b, scale, norm)
    dpartial = lax.map(one_block, (blocks, label_blocks))
    dpartial = dpartial.transpose(1, 0, 2, 3).reshape(layers, TOKENS, CLASSES)

    def weight_grad(pair):
        return jnp.dot(pair[0].T, pair[1], preferred_element_type=jnp.float32)
    return lax.map(weight_grad, (acts, dpartial))
```

```python
import functools
import math

import jax
import jax.numpy as jnp
from jax import lax
from jax.experimental import pallas as pl
from jax.experimental.pallas import tpu as pltpu
from jax.sharding import PartitionSpec as P

MESH = pl.DeviceIdType.MESH
WIRE = jnp.int16
STEPS = 32767.0
SUB = 64
LANES = 128


def flip(value, bit):
    return value + bit - 2 * bit * ((value // bit) % 2)


def kernel(dims, table, scale, labels, acts, weight, out, acts_v, w_v, wire, got, wire_step, got_step, ret, dp, far_acts, far_dp, acc, rs_out, rs_in,
           s_acts, s_w, f_send, f_recv, g_send, g_recv, b_send, b_recv, a_send, a_recv, d_send, d_recv, r_send, r_recv):
    layers, subs, chips, stages, rows, width, classes, norm = dims
    each = rows // layers
    block = width // (2 * chips)
    me = lax.axis_index("layer")
    tok = lax.axis_index("tok")
    core = tok % 2
    chip = tok // 2
    mate = tok + 1 - 2 * core

    def load_acts(s, l):
        return pltpu.make_async_copy(
            acts.at[0, pl.ds(l * each + s * SUB, SUB), :], acts_v.at[s, pl.ds(l * SUB, SUB), :], s_acts.at[s, l]
        )

    load_w = pltpu.make_async_copy(weight.at[0], w_v, s_w)
    for l in range(layers):
        load_acts(0, l).start()
    load_w.start()
    for s in range(1, subs):
        for l in range(layers):
            load_acts(s, l).start()

    bits = []
    for i in range(stages):
        low, high = 2 ** i, 2 ** (stages - 1 - i)
        bits.append(low + core * (high - low))

    def chip_of(mask):
        where = chip
        for i in range(stages):
            if mask & (1 << i):
                where = flip(where, bits[i])
        return where

    peers = [lax.rem(me + k, layers) for k in sorted(range(1, layers), key=lambda k: abs(k - layers // 2))]
    barrier = pltpu.get_barrier_semaphore()
    for peer in peers:
        pl.semaphore_signal(barrier, inc=1, device_id=(peer, tok), device_id_type=MESH)
    pl.semaphore_signal(barrier, inc=1, device_id=(me, mate), device_id_type=MESH)
    for i in range(stages):
        pl.semaphore_signal(barrier, inc=1, device_id=(me, flip(chip, bits[i]) * 2 + core), device_id_type=MESH)

    def pair_step(q, totals):
        a, b, c = table[q, 0], table[q, 1], scale[q]
        new = []
        at = 0
        for l in range(layers):
            for m in range(l, layers):
                one = jnp.where((a == l) & (b == m), c, 0.0) + jnp.where((a == m) & (b == l), c, 0.0)
                new.append(totals[at] + one)
                at += 1
        return tuple(new)

    flat = lax.fori_loop(0, table.shape[0], pair_step, (jnp.float32(0.0),) * (layers * (layers + 1) // 2))
    mix = [[None] * layers for _ in range(layers)]
    at = 0
    for l in range(layers):
        for m in range(l, layers):
            mix[l][m] = mix[m][l] = flat[at]
            at += 1

    pl.semaphore_wait(barrier, layers - 1 + 1 + stages)

    def fwd_copy(s, peer):
        return pltpu.make_async_remote_copy(
            src_ref=wire.at[s, peer], dst_ref=got.at[s, me], send_sem=f_send.at[s, peer], recv_sem=f_recv.at[s, me],
            device_id=(peer, tok), device_id_type=MESH)

    def fwd_arrival(s, peer):
        return pltpu.make_async_remote_copy(
            src_ref=wire.at[s, peer], dst_ref=got.at[s, peer], send_sem=f_send.at[s, peer], recv_sem=f_recv.at[s, peer],
            device_id=(peer, tok), device_id_type=MESH)

    def step_copy(s, peer):
        return pltpu.make_async_remote_copy(
            src_ref=wire_step.at[s, peer], dst_ref=got_step.at[s, me], send_sem=g_send.at[s, peer], recv_sem=g_recv.at[s, me],
            device_id=(peer, tok), device_id_type=MESH)

    def step_arrival(s, peer):
        return pltpu.make_async_remote_copy(
            src_ref=wire_step.at[s, peer], dst_ref=got_step.at[s, peer], send_sem=g_send.at[s, peer], recv_sem=g_recv.at[s, peer],
            device_id=(peer, tok), device_id_type=MESH)

    def ret_copy(s, peer):
        return pltpu.make_async_remote_copy(
            src_ref=ret.at[s, peer], dst_ref=dp.at[s, pl.ds(me * SUB, SUB), :], send_sem=b_send.at[s, peer], recv_sem=b_recv.at[s, me],
            device_id=(peer, tok), device_id_type=MESH)

    def ret_arrival(s, peer):
        return pltpu.make_async_remote_copy(
            src_ref=ret.at[s, peer], dst_ref=dp.at[s, pl.ds(peer * SUB, SUB), :], send_sem=b_send.at[s, peer], recv_sem=b_recv.at[s, peer],
            device_id=(peer, tok), device_id_type=MESH)

    def cols(c, of_core):
        return pl.ds(pl.multiple_of((c * 2 + of_core) * block, block), block)

    def acts_copy(s, c):
        return pltpu.make_async_remote_copy(
            src_ref=acts_v.at[s, :, cols(c, 1 - core)], dst_ref=far_acts.at[s, c], send_sem=a_send.at[s, c], recv_sem=a_recv.at[s, c],
            device_id=(me, mate), device_id_type=MESH)

    def dp_copy(s):
        return pltpu.make_async_remote_copy(
            src_ref=dp.at[s], dst_ref=far_dp.at[s], send_sem=d_send.at[s], recv_sem=d_recv.at[s],
            device_id=(me, mate), device_id_type=MESH)

    load_w.wait()
    lane = lax.broadcasted_iota(jnp.int32, (SUB, LANES), 1)
    row = lax.broadcasted_iota(jnp.int32, (SUB, LANES), 0)

    def forward(s, _):
        for l in range(layers):
            load_acts(s, l).wait()
        part = jnp.dot(acts_v[s], w_v[...], preferred_element_type=jnp.float32)
        for l in range(layers):
            here = part[l * SUB:(l + 1) * SUB]
            reach = jnp.maximum(jnp.max(jnp.abs(here), axis=1, keepdims=True), 1e-30)
            wire[s, l] = jnp.round(here * (STEPS / reach)).astype(jnp.int32).astype(WIRE)
            spread = jnp.where(lane == row, jnp.broadcast_to(reach * (1.0 / STEPS), (SUB, LANES)), 0.0)
            wire_step[s, l] = jnp.sum(spread, axis=0, keepdims=True)
        for peer in peers:
            step_copy(s, peer).start()
            fwd_copy(s, peer).start()
        for c in range(chips):
            acts_copy(s, c).start()
        got[s, me] = wire[s, me]
        got_step[s, me] = wire_step[s, me]
        return 0

    lax.fori_loop(0, subs, forward, 0)

    span = lax.broadcasted_iota(jnp.int32, (SUB, classes), 1).astype(jnp.float32)

    def score(s, _):
        for peer in peers:
            fwd_arrival(s, peer).wait_recv()
            step_arrival(s, peer).wait_recv()
        first = me * each + s * SUB


        def column(line, shift):
            picked = jnp.where(lane == row + shift, jnp.broadcast_to(line, (SUB, LANES)), 0.0)
            return jnp.sum(picked, axis=1, keepdims=True)

        label = column(labels[pl.ds(first // LANES, 1), :].astype(jnp.float32), first % LANES)
        values = [got[s, l].astype(jnp.int32).astype(jnp.float32) * column(got_step[s, l], 0) for l in range(layers)]
        factors = []
        logits = None
        for l in range(layers):
            total = values[0] * mix[l][0]
            for m in range(1, layers):
                total = total + values[m] * mix[l][m]
            term = values[l] * (1.0 + 0.5 * total)
            logits = term if logits is None else logits + term
            factors.append(1.0 + total)
        top = jnp.max(logits, axis=1, keepdims=True)
        expo = jnp.exp(logits - top)
        probs = expo * (1.0 / jnp.sum(expo, axis=1, keepdims=True))
        grad = (probs - jnp.where(span == label, 1.0, 0.0)) * norm
        for l in range(layers):
            ret[s, l] = (grad * factors[l]).astype(jnp.bfloat16)
        for peer in peers:
            ret_copy(s, peer).start()
        dp[s, pl.ds(me * SUB, SUB), :] = ret[s, me]
        return 0

    lax.fori_loop(0, subs, score, 0)

    def product(s, mask):
        c = chip_of(mask)
        dims_ = (((0,), (0,)), ((), ()))
        near = lax.dot_general(acts_v[s, :, cols(c, core)], dp[s], dims_, preferred_element_type=jnp.float32)
        far = lax.dot_general(far_acts[s, c], far_dp[s], dims_, preferred_element_type=jnp.float32)
        return near + far

    def arrive(s):
        for peer in peers:
            ret_arrival(s, peer).wait_recv()
        dp_copy(s).start()
        for c in range(chips):
            acts_copy(s, c).wait_recv()
        dp_copy(s).wait_recv()

    for mask in range(chips):
        acc[mask] = jnp.zeros((block, classes), jnp.float32)

    def backward(s, _):
        arrive(s)
        for mask in range(chips):
            acc[mask] += product(s, mask)
        return 0

    lax.fori_loop(0, subs - 1, backward, 0)

    def low_bit(mask):
        return (mask & -mask).bit_length() - 1 if mask else stages

    def rs_copy(mask):
        i = low_bit(mask)
        return pltpu.make_async_remote_copy(
            src_ref=rs_out.at[mask - 1], dst_ref=rs_in.at[mask - 1], send_sem=r_send.at[mask - 1], recv_sem=r_recv.at[mask - 1],
            device_id=(me, flip(chip, bits[i]) * 2 + core), device_id_type=MESH)

    last = subs - 1
    arrive(last)
    order = sorted(range(chips), key=lambda mask: (low_bit(mask), -mask))
    waiting = []
    for mask in order:
        total = acc[mask] + product(last, mask)
        if low_bit(mask) == 0:
            rs_out[mask - 1] = total.astype(jnp.bfloat16)
            rs_copy(mask).start()
        else:
            acc[mask] = total
            waiting.append(mask)
    for mask in waiting:
        total = acc[mask]
        for i in range(low_bit(mask)):
            other = mask + (1 << i)
            rs_copy(other).wait_recv()
            total = total + rs_in[other - 1].astype(jnp.float32)
        if mask:
            rs_out[mask - 1] = total.astype(jnp.bfloat16)
            rs_copy(mask).start()
        else:
            out[0] = total

    def finish(s, _):
        for peer in peers:
            fwd_copy(s, peer).wait_send()
            step_copy(s, peer).wait_send()
            ret_copy(s, peer).wait_send()
        for c in range(chips):
            acts_copy(s, c).wait_send()
        dp_copy(s).wait_send()
        return 0

    lax.fori_loop(0, subs, finish, 0)
    for mask in range(1, chips):
        rs_copy(mask).wait_send()


def local(groups, toks, acts, probe_weight, mix_table, mix_scale, labels):
    _, rows, width = acts.shape
    classes = probe_weight.shape[2]
    each = rows // groups
    subs = each // SUB
    chips = toks // 2
    stages = chips.bit_length() - 1
    block = width // toks
    norm = 1.0 / math.sqrt(rows * toks)
    dims = (groups, subs, chips, stages, rows, width, classes, norm)
    mixed = groups * SUB
    dma = pltpu.SemaphoreType.DMA
    bf16 = jnp.bfloat16
    vmem = pl.BlockSpec(memory_space=pltpu.VMEM)
    smem = pl.BlockSpec(memory_space=pltpu.SMEM)
    hbm = pl.BlockSpec(memory_space=pl.ANY)
    return pl.pallas_call(
        functools.partial(kernel, dims),
        out_shape=jax.ShapeDtypeStruct((1, block, classes), jnp.float32),
        in_specs=[smem, smem, vmem, hbm, hbm],
        out_specs=vmem,
        scratch_shapes=[
            pltpu.VMEM((subs, mixed, width), bf16),
            pltpu.VMEM((width, classes), bf16),
            pltpu.VMEM((subs, groups, SUB, classes), WIRE),
            pltpu.VMEM((subs, groups, SUB, classes), WIRE),
            pltpu.VMEM((subs, groups, 1, LANES), jnp.float32),
            pltpu.VMEM((subs, groups, 1, LANES), jnp.float32),
            pltpu.VMEM((subs, groups, SUB, classes), bf16),
            pltpu.VMEM((subs, mixed, classes), bf16),
            pltpu.VMEM((subs, chips, mixed, block), bf16),
            pltpu.VMEM((subs, mixed, classes), bf16),
            pltpu.VMEM((chips, block, classes), jnp.float32),
            pltpu.VMEM((chips - 1, block, classes), bf16),
            pltpu.VMEM((chips - 1, block, classes), bf16),
            dma((subs, groups)), dma,
            dma((subs, groups)), dma((subs, groups)),
            dma((subs, groups)), dma((subs, groups)),
            dma((subs, groups)), dma((subs, groups)),
            dma((subs, chips)), dma((subs, chips)),
            dma((subs,)), dma((subs,)),
            dma((chips - 1,)), dma((chips - 1,)),
        ],
        compiler_params=pltpu.CompilerParams(collective_id=0, has_side_effects=True, vmem_limit_bytes=60 * 1024 * 1024),
    )(mix_table, mix_scale, labels.reshape(rows // LANES, LANES), acts, probe_weight)


def solution(mesh):
    in_specs = (P("layer", "tok", None), P("layer", None, None), P(), P(), P("tok"))
    out_specs = P("layer", "tok", None)
    body = functools.partial(local, mesh.shape["layer"], mesh.shape["tok"])
    return jax.shard_map(body, mesh=mesh, in_specs=in_specs, out_specs=out_specs, check_vma=False)
```

```python
import functools
import math

import jax
import jax.numpy as jnp
from jax import lax
from jax.experimental import pallas as pl
from jax.experimental.pallas import tpu as pltpu
from jax.sharding import PartitionSpec as P

MESH = pl.DeviceIdType.MESH
WIRE = jnp.int16
STEPS = 32767.0
SUB = 64
SLABS = 4
LANES = 128


def flip(value, bit):
    return value + bit - 2 * bit * ((value // bit) % 2)


def kernel(dims, table, scale, labels, acts, weight, out, acts_v, w_v, wire, got, wire_step, got_step, ret, dp, far_acts, far_dp, acc, rs_out, rs_in,
           s_acts, s_slab, s_w, f_send, f_recv, g_send, g_recv, b_send, b_recv, a_send, a_recv, d_send, d_recv, r_send, r_recv):
    layers, subs, chips, stages, rows, width, classes, norm = dims
    each = rows // layers
    block = width // (2 * chips)
    me = lax.axis_index("layer")
    tok = lax.axis_index("tok")
    core = tok % 2
    chip = tok // 2
    mate = tok + 1 - 2 * core

    def load_acts(s, l):
        return pltpu.make_async_copy(
            acts.at[0, pl.ds(l * each + s * SUB, SUB), :], acts_v.at[s, pl.ds(l * SUB, SUB), :], s_acts.at[s, l]
        )

    deep = width // SLABS

    def load_slab(k):
        span_k = pl.ds(k * deep, deep)
        parts = [pltpu.make_async_copy(
            acts.at[0, pl.ds(l * each, SUB), span_k], acts_v.at[0, pl.ds(l * SUB, SUB), span_k], s_slab.at[k, l]
        ) for l in range(layers)]
        return parts + [pltpu.make_async_copy(weight.at[0, span_k, :], w_v.at[span_k, :], s_w.at[k])]

    for k in range(SLABS):
        for load in load_slab(k):
            load.start()

    bits = []
    for i in range(stages):
        low, high = 2 ** i, 2 ** (stages - 1 - i)
        bits.append(low + core * (high - low))

    def chip_of(mask):
        where = chip
        for i in range(stages):
            if mask & (1 << i):
                where = flip(where, bits[i])
        return where

    def other_layer(k):
        where = me
        for i in range((layers - 1).bit_length()):
            if k & (1 << i):
                where = flip(where, 1 << i)
        return where

    peers = [other_layer(k) for k in range(layers - 1, 0, -1)]
    barrier = pltpu.get_barrier_semaphore()
    for peer in peers:
        pl.semaphore_signal(barrier, inc=1, device_id=(peer, tok), device_id_type=MESH)
    pl.semaphore_signal(barrier, inc=1, device_id=(me, mate), device_id_type=MESH)
    for i in range(stages):
        pl.semaphore_signal(barrier, inc=1, device_id=(me, flip(chip, bits[i]) * 2 + core), device_id_type=MESH)

    def pair_step(q, totals):
        a, b, c = table[0, q], table[1, q], scale[q]
        new = []
        at = 0
        for l in range(layers):
            for m in range(l, layers):
                one = jnp.where((a == l) & (b == m), c, 0.0) + jnp.where((a == m) & (b == l), c, 0.0)
                new.append(totals[at] + one)
                at += 1
        return tuple(new)

    flat = lax.fori_loop(0, table.shape[1], pair_step, (jnp.float32(0.0),) * (layers * (layers + 1) // 2))
    mix = [[None] * layers for _ in range(layers)]
    at = 0
    for l in range(layers):
        for m in range(l, layers):
            mix[l][m] = mix[m][l] = flat[at]
            at += 1

    pl.semaphore_wait(barrier, layers - 1 + 1 + stages)

    def fwd_copy(s, peer):
        return pltpu.make_async_remote_copy(
            src_ref=wire.at[s, peer], dst_ref=got.at[s, me], send_sem=f_send.at[s, peer], recv_sem=f_recv.at[s, me],
            device_id=(peer, tok), device_id_type=MESH)

    def fwd_arrival(s, peer):
        return pltpu.make_async_remote_copy(
            src_ref=wire.at[s, peer], dst_ref=got.at[s, peer], send_sem=f_send.at[s, peer], recv_sem=f_recv.at[s, peer],
            device_id=(peer, tok), device_id_type=MESH)

    def step_copy(s, peer):
        return pltpu.make_async_remote_copy(
            src_ref=wire_step.at[s, peer], dst_ref=got_step.at[s, me], send_sem=g_send.at[s, peer], recv_sem=g_recv.at[s, me],
            device_id=(peer, tok), device_id_type=MESH)

    def step_arrival(s, peer):
        return pltpu.make_async_remote_copy(
            src_ref=wire_step.at[s, peer], dst_ref=got_step.at[s, peer], send_sem=g_send.at[s, peer], recv_sem=g_recv.at[s, peer],
            device_id=(peer, tok), device_id_type=MESH)

    def ret_copy(s, peer):
        return pltpu.make_async_remote_copy(
            src_ref=ret.at[s, peer], dst_ref=dp.at[s, pl.ds(me * SUB, SUB), :], send_sem=b_send.at[s, peer], recv_sem=b_recv.at[s, me],
            device_id=(peer, tok), device_id_type=MESH)

    def ret_arrival(s, peer):
        return pltpu.make_async_remote_copy(
            src_ref=ret.at[s, peer], dst_ref=dp.at[s, pl.ds(peer * SUB, SUB), :], send_sem=b_send.at[s, peer], recv_sem=b_recv.at[s, peer],
            device_id=(peer, tok), device_id_type=MESH)

    def cols(c, of_core):
        return pl.ds(pl.multiple_of((c * 2 + of_core) * block, block), block)

    def acts_copy(s, c):
        return pltpu.make_async_remote_copy(
            src_ref=acts_v.at[s, :, cols(c, 1 - core)], dst_ref=far_acts.at[s, c], send_sem=a_send.at[s, c], recv_sem=a_recv.at[s, c],
            device_id=(me, mate), device_id_type=MESH)

    def dp_copy(s, l):
        piece = pl.ds(l * SUB, SUB)
        return pltpu.make_async_remote_copy(
            src_ref=dp.at[s, piece, :], dst_ref=far_dp.at[s, piece, :], send_sem=d_send.at[s, l], recv_sem=d_recv.at[s, l],
            device_id=(me, mate), device_id_type=MESH)

    lane = lax.broadcasted_iota(jnp.int32, (SUB, LANES), 1)
    row = lax.broadcasted_iota(jnp.int32, (SUB, LANES), 0)

    def send_logits(s, part):
        for l in range(layers):
            here = part[l * SUB:(l + 1) * SUB]
            reach = jnp.maximum(jnp.max(jnp.abs(here), axis=1, keepdims=True), 1e-30)
            wire[s, l] = jnp.round(here * (STEPS / reach)).astype(jnp.int32).astype(WIRE)
            spread = jnp.where(lane == row, jnp.broadcast_to(reach * (1.0 / STEPS), (SUB, LANES)), 0.0)
            wire_step[s, l] = jnp.sum(spread, axis=0, keepdims=True)
        for peer in peers:
            step_copy(s, peer).start()
            fwd_copy(s, peer).start()
        for c in range(chips):
            acts_copy(s, c).start()
        got[s, me] = wire[s, me]
        got_step[s, me] = wire_step[s, me]

    part = None
    for k in range(SLABS):
        for load in load_slab(k):
            load.wait()
        span_k = pl.ds(k * deep, deep)
        term = jnp.dot(acts_v[0, :, span_k], w_v[span_k, :], preferred_element_type=jnp.float32)
        part = term if part is None else part + term
        if k == SLABS - 2:
            for s in range(1, subs):
                for l in range(layers):
                    load_acts(s, l).start()
    send_logits(0, part)

    def forward(s, _):
        for l in range(layers):
            load_acts(s, l).wait()
        send_logits(s, jnp.dot(acts_v[s], w_v[...], preferred_element_type=jnp.float32))
        return 0

    lax.fori_loop(1, subs, forward, 0)

    span = lax.broadcasted_iota(jnp.int32, (SUB, classes), 1).astype(jnp.float32)

    def score(s, _):
        for peer in peers:
            fwd_arrival(s, peer).wait_recv()
            step_arrival(s, peer).wait_recv()
        first = me * each + s * SUB


        def column(line, shift):
            picked = jnp.where(lane == row + shift, jnp.broadcast_to(line, (SUB, LANES)), 0.0)
            return jnp.sum(picked, axis=1, keepdims=True)

        label = column(labels[pl.ds(first // LANES, 1), :].astype(jnp.float32), first % LANES)
        values = [got[s, l].astype(jnp.int32).astype(jnp.float32) * column(got_step[s, l], 0) for l in range(layers)]
        factors = []
        logits = None
        for l in range(layers):
            total = values[0] * mix[l][0]
            for m in range(1, layers):
                total = total + values[m] * mix[l][m]
            term = values[l] * (1.0 + 0.5 * total)
            logits = term if logits is None else logits + term
            factors.append(1.0 + total)
        top = jnp.max(logits, axis=1, keepdims=True)
        expo = jnp.exp(logits - top)
        probs = expo * (1.0 / jnp.sum(expo, axis=1, keepdims=True))
        grad = (probs - jnp.where(span == label, 1.0, 0.0)) * norm
        for l in range(layers):
            ret[s, l] = (grad * factors[l]).astype(jnp.bfloat16)
        for peer in peers:
            ret_copy(s, peer).start()
        dp[s, pl.ds(me * SUB, SUB), :] = ret[s, me]
        dp_copy(s, me).start()
        return 0

    lax.fori_loop(0, subs, score, 0)

    contract = (((0,), (0,)), ((), ()))

    def near(s, mask):
        return lax.dot_general(acts_v[s, :, cols(chip_of(mask), core)], dp[s], contract, preferred_element_type=jnp.float32)

    def far(s, mask):
        return lax.dot_general(far_acts[s, chip_of(mask)], far_dp[s], contract, preferred_element_type=jnp.float32)

    def arrive(s):
        for peer in peers[::-1]:
            ret_arrival(s, peer).wait_recv()
            dp_copy(s, peer).start()

    def arrive_far(s):
        for c in range(chips):
            acts_copy(s, c).wait_recv()
        for l in range(layers):
            dp_copy(s, l).wait_recv()

    for mask in range(chips):
        acc[mask] = jnp.zeros((block, classes), jnp.float32)

    def backward(s, _):
        arrive(s)
        for mask in range(chips):
            acc[mask] += near(s, mask)
        arrive_far(s)
        for mask in range(chips):
            acc[mask] += far(s, mask)
        return 0

    lax.fori_loop(0, subs - 1, backward, 0)

    def low_bit(mask):
        return (mask & -mask).bit_length() - 1 if mask else stages

    def rs_copy(mask):
        i = low_bit(mask)
        return pltpu.make_async_remote_copy(
            src_ref=rs_out.at[mask - 1], dst_ref=rs_in.at[mask - 1], send_sem=r_send.at[mask - 1], recv_sem=r_recv.at[mask - 1],
            device_id=(me, flip(chip, bits[i]) * 2 + core), device_id_type=MESH)

    last = subs - 1
    arrive(last)
    for mask in range(chips):
        acc[mask] += near(last, mask)
    arrive_far(last)
    order = sorted(range(chips), key=lambda mask: (low_bit(mask), -mask))
    waiting = []
    for mask in order:
        total = acc[mask] + far(last, mask)
        if low_bit(mask) == 0:
            rs_out[mask - 1] = total.astype(jnp.bfloat16)
            rs_copy(mask).start()
        else:
            acc[mask] = total
            waiting.append(mask)
    for mask in waiting:
        total = acc[mask]
        for i in range(low_bit(mask)):
            other = mask + (1 << i)
            rs_copy(other).wait_recv()
            total = total + rs_in[other - 1].astype(jnp.float32)
        if mask:
            rs_out[mask - 1] = total.astype(jnp.bfloat16)
            rs_copy(mask).start()
        else:
            out[0] = total

    def finish(s, _):
        for peer in peers:
            fwd_copy(s, peer).wait_send()
            step_copy(s, peer).wait_send()
            ret_copy(s, peer).wait_send()
        for c in range(chips):
            acts_copy(s, c).wait_send()
        for l in range(layers):
            dp_copy(s, l).wait_send()
        return 0

    lax.fori_loop(0, subs, finish, 0)
    for mask in range(1, chips):
        rs_copy(mask).wait_send()


def local(groups, toks, acts, probe_weight, mix_table, mix_scale, labels):
    _, rows, width = acts.shape
    classes = probe_weight.shape[2]
    each = rows // groups
    subs = each // SUB
    chips = toks // 2
    stages = chips.bit_length() - 1
    block = width // toks
    norm = 1.0 / math.sqrt(rows * toks)
    dims = (groups, subs, chips, stages, rows, width, classes, norm)
    mixed = groups * SUB
    dma = pltpu.SemaphoreType.DMA
    bf16 = jnp.bfloat16
    vmem = pl.BlockSpec(memory_space=pltpu.VMEM)
    smem = pl.BlockSpec(memory_space=pltpu.SMEM)
    hbm = pl.BlockSpec(memory_space=pl.ANY)
    return pl.pallas_call(
        functools.partial(kernel, dims),
        out_shape=pltpu.VMEM((1, block, classes), jnp.float32),
        in_specs=[smem, smem, vmem, hbm, hbm],
        out_specs=vmem,
        scratch_shapes=[
            pltpu.VMEM((subs, mixed, width), bf16),
            pltpu.VMEM((width, classes), bf16),
            pltpu.VMEM((subs, groups, SUB, classes), WIRE),
            pltpu.VMEM((subs, groups, SUB, classes), WIRE),
            pltpu.VMEM((subs, groups, 1, LANES), jnp.float32),
            pltpu.VMEM((subs, groups, 1, LANES), jnp.float32),
            pltpu.VMEM((subs, groups, SUB, classes), bf16),
            pltpu.VMEM((subs, mixed, classes), bf16),
            pltpu.VMEM((subs, chips, mixed, block), bf16),
            pltpu.VMEM((subs, mixed, classes), bf16),
            pltpu.VMEM((chips, block, classes), jnp.float32),
            pltpu.VMEM((chips - 1, block, classes), bf16),
            pltpu.VMEM((chips - 1, block, classes), bf16),
            dma((subs, groups)), dma((SLABS, groups)), dma((SLABS,)),
            dma((subs, groups)), dma((subs, groups)),
            dma((subs, groups)), dma((subs, groups)),
            dma((subs, groups)), dma((subs, groups)),
            dma((subs, chips)), dma((subs, chips)),
            dma((subs, groups)), dma((subs, groups)),
            dma((chips - 1,)), dma((chips - 1,)),
        ],
        compiler_params=pltpu.CompilerParams(collective_id=0, has_side_effects=True, vmem_limit_bytes=60 * 1024 * 1024),
    )(mix_table.T, mix_scale, labels.reshape(rows // LANES, LANES), acts, probe_weight)


def solution(mesh):
    in_specs = (P("layer", "tok", None), P("layer", None, None), P(), P(), P("tok"))
    out_specs = P("layer", "tok", None)
    body = functools.partial(local, mesh.shape["layer"], mesh.shape["tok"])
    return jax.shard_map(body, mesh=mesh, in_specs=in_specs, out_specs=out_specs, check_vma=False)
```
